32 devices in a mesh: dp: 4 (over z), group: 8 (over y, x, core).
Axes of the slice: x: 2, y: 2, z: 4, core: 2. Of those that a mesh axis runs over, the one named last changes fastest.
Arguments:
- query: bfloat16 [4096, 4096], P(('dp', 'group')), may hold values from -6 to 6
- comp_key: bfloat16 [4096, 512], P(('dp', 'group')), may hold values from -6 to 6
- comp_value: bfloat16 [4096, 512], P(('dp', 'group')), may hold values from -6 to 6
- prompt_key: bfloat16 [128, 512], P(('dp', 'group')), may hold values from -6 to 6
- prompt_value: bfloat16 [128, 512], P(('dp', 'group')), may hold values from -6 to 6
- d_out: bfloat16 [4096, 4096], P(('dp', 'group')), may hold values from -6 to 6
- q_gain: float32 [128], replicated, may hold values from 0.5 to 1.5
- k_gain: float32 [128], replicated, may hold values from 0.5 to 1.5
- lengths: int32 [32], P(('dp', 'group')), may hold values from 1 to 128, 2560 in all
Outputs:
- d_query: bfloat16 [4096, 4096], P(('dp', 'group'))
- d_comp_key: bfloat16 [4096, 512], P(('dp', 'group'))
- d_comp_value: bfloat16 [4096, 512], P(('dp', 'group'))
- d_prompt_key: bfloat16 [128, 512], P(('dp', 'group'))
- d_prompt_value: bfloat16 [128, 512], P(('dp', 'group'))
- d_q_gain: float32 [128], replicated
- d_k_gain: float32 [128], replicated
The draws below stay inside these ranges and needn't reach their ends.
Inputs may be any that keep to these rules, and one draw needn't show every extreme that they name: `lengths`: each entry is the live slots of one completion, at most 128; some completion has exactly 128.
All inputs are finite; a program needn't handle non-finite values. No bound on the sum of `lengths` on one device may be relied on, other than what follows from the above.
Results may differ from the reference program's by a relative error of at most 0.025.
Values may be sent and summed in bfloat16 or wider, within the bound.
A program may use at most 64 MiB of HBM per device.

```python
import math
import jax
import jax.numpy as jnp
import numpy as np
from jax import lax

HD = 128
HQ = 32
HK = 4
C_DEV = 128
PROMPT = 32
SAMPLES = 32
COMP_TOK = 4096
PROMPT_TOK = 128
N_DP = 4
N_GROUP = 8


def block_levels(key, extent, cuts, least, top_value):
    loudness = 1.0
    for dim, blocks in cuts:
        draws = jax.random.uniform(jax.random.fold_in(jax.random.fold_in(key, 6), dim), (blocks,), jnp.float32, least / len(cuts), top_value / len(cuts))
        loudness = loudness * jnp.repeat(jnp.exp(draws), extent[dim] // blocks).reshape((-1,) + (1,) * (len(extent) - 1 - dim))
    return loudness


def profile(number_of, total, bound, skew):
    loads = [(1 << 20) // math.isqrt(grade ** skew) + 1 for grade in range(2, number_of + 1)]
    spare, counts = total - bound - (number_of - 1), [1] * (number_of - 1)
    while spare > 0:
        free = [i for i in range(number_of - 1) if counts[i] < bound]
        mass, left = sum([loads[i] for i in free]), spare
        for i in free:
            addition = min(bound - counts[i], max(1, left * loads[i] // mass), spare)
            counts[i] = counts[i] + addition
            spare = spare - addition
    return np.array([bound] + counts)


def ragged_sizes(own_key, amount, total, bound, lean):
    if amount == 2:
        one = jax.random.randint(own_key, (), max(1, total - bound), min(bound, total - 1) + 1)
        return jnp.stack([one, total - one])
    sizes = jnp.asarray(profile(amount, total, bound, lean), jnp.int32)
    couples = (amount - 1) // 2
    giver, sink = sizes[1:1 + 2 * couples:2], sizes[2:2 + 2 * couples:2]
    slack = jnp.minimum(giver - 1, bound - sink)
    moved = jax.random.randint(jax.random.fold_in(own_key, 1), (couples,), 0, 1 << 20) % (slack + 1)
    sizes = sizes.at[1:1 + 2 * couples:2].set(giver - moved).at[2:2 + 2 * couples:2].set(sink + moved)
    return sizes[jax.random.permutation(jax.random.fold_in(own_key, 2), amount)]


def normal_values(own_key, dims, deviation, bound, shards=(), kind=jnp.bfloat16):
    values = jax.random.normal(own_key, dims, jnp.float32) * deviation
    if len(shards) > 0:
        values = block_levels(own_key, dims, shards, -0.22, 0.18) * values
    return jnp.clip(values, min=-bound, max=bound).astype(kind)


def setup_inputs(seed: int = 0) -> dict:
    streams_of = jax.random.split(jax.random.key(seed), 10)
    query = normal_values(streams_of[0], (COMP_TOK, HQ * HD), 1.0, 6.0, ((0, 32),))
    comp_key = normal_values(streams_of[1], (COMP_TOK, HK * HD), 1.0, 6.0, ((0, 32),))
    comp_value = normal_values(streams_of[2], (COMP_TOK, HK * HD), 1.0, 6.0, ((0, 32),))
    prompt_key = normal_values(streams_of[3], (PROMPT_TOK, HK * HD), 1.0, 6.0, ((0, 32),))
    prompt_value = normal_values(streams_of[4], (PROMPT_TOK, HK * HD), 1.0, 6.0, ((0, 32),))
    d_out = normal_values(streams_of[5], (COMP_TOK, HQ * HD), 1.0, 6.0, ((0, 32),))
    q_gain = jnp.clip(1.0 + 0.1 * jax.random.normal(streams_of[6], (HD,), jnp.float32), 0.5, 1.5)
    k_gain = jnp.clip(1.0 + 0.1 * jax.random.normal(streams_of[7], (HD,), jnp.float32), 0.5, 1.5)
    lengths = ragged_sizes(streams_of[8], SAMPLES, SAMPLES * C_DEV * 5 // 8, C_DEV, 2).astype(jnp.int32)
    return {"query": query, "comp_key": comp_key, "comp_value": comp_value, "prompt_key": prompt_key, "prompt_value": prompt_value, "d_out": d_out, "q_gain": q_gain, "k_gain": k_gain, "lengths": lengths}


EPS = 1e-06

def widen(value):
    return lax.optimization_barrier(value).astype(jnp.float32)

def normalize(vectors, gain):
    wide = vectors.astype(jnp.float32)
    inverse = lax.rsqrt(lax.optimization_barrier(jnp.mean(wide * wide, axis=-1, keepdims=True)) + EPS)
    unit = wide * inverse
    return ((unit * gain).astype(jnp.bfloat16), unit, inverse)

def norm_back(grad, unit, inverse, gain):
    scaled = grad * gain
    back = inverse * (scaled - unit * lax.optimization_barrier(jnp.mean(scaled * unit, axis=-1, keepdims=True)))
    return (back, lax.optimization_barrier(jnp.sum((grad * unit).reshape(-1, unit.shape[-1]), axis=0)))

def attend_back(normed_query, keys, values, grad_out, visible):
    count = normed_query.shape[0]
    groups = HQ // HK
    scale = HD ** (-0.5)
    query_four = widen(normed_query).reshape(count, HK, groups, HD)
    keys_wide = widen(keys)
    values_wide = values.astype(jnp.float32)
    grad_four = grad_out.astype(jnp.float32).reshape(count, HK, groups, HD)
    scores = jnp.einsum('chgd,khd->hgck', query_four, keys_wide) * scale
    expo = jnp.where(visible, jnp.exp(scores), 0.0)
    probs = expo / lax.optimization_barrier(jnp.sum(expo, axis=-1, keepdims=True))
    rounded = widen(probs.astype(jnp.bfloat16))
    output = jnp.einsum('hgck,khd->chgd', rounded, values_wide)
    delta = jnp.transpose(lax.optimization_barrier(jnp.sum(grad_four * output, axis=-1)), (1, 2, 0))[..., None]
    dprob = jnp.einsum('chgd,khd->hgck', grad_four, values_wide)
    dscore = widen((probs * (dprob - delta)).astype(jnp.bfloat16))
    dquery = (jnp.einsum('hgck,khd->chgd', dscore, keys_wide) * scale).reshape(count, HQ, HD)
    dkey = jnp.einsum('hgck,chgd->khd', dscore, query_four) * scale
    dvalue = jnp.einsum('hgck,chgd->khd', rounded, grad_four)
    return (dquery, dkey, dvalue)

def reference(query, comp_key, comp_value, prompt_key, prompt_value, d_out, q_gain, k_gain, lengths):
    count = C_DEV
    width_q = HQ * HD
    width_k = HK * HD
    rows = jnp.arange(count, dtype=jnp.int32)
    visible = jnp.concatenate([jnp.ones((count, PROMPT), bool), rows[None, :] <= rows[:, None]], axis=1)

    def one_prompt(items):
        pkey, pvalue, queries, ckeys, cvalues, grads, lens = items
        pnorm, punit, pinv = normalize(pkey.reshape(PROMPT, HK, HD), k_gain)
        pvals = pvalue.reshape(PROMPT, HK, HD)

        def one_sample(carry, sample):
            key_acc, value_acc, gain_query, gain_key = carry
            qrow, krow, vrow, grow, length = sample
            qnorm, qunit, qinv = normalize(qrow.reshape(count, HQ, HD), q_gain)
            cnorm, cunit, cinv = normalize(krow.reshape(count, HK, HD), k_gain)
            live = (rows < length)[:, None]
            masked = jnp.where(live, grow, jnp.zeros_like(grow))
            keys = jnp.concatenate([pnorm, cnorm], axis=0)
            values = jnp.concatenate([pvals, vrow.reshape(count, HK, HD)], axis=0)
            dquery, dkey, dvalue = attend_back(qnorm, keys, values, masked.reshape(count, HQ, HD), visible)
            dq, gq = norm_back(dquery, qunit, qinv, q_gain)
            dck, gk = norm_back(dkey[PROMPT:], cunit, cinv, k_gain)
            carry = (key_acc + dkey[:PROMPT], value_acc + dvalue[:PROMPT], gain_query + gq, gain_key + gk)
            emitted = (dq.reshape(count, width_q).astype(jnp.bfloat16), dck.reshape(count, width_k).astype(jnp.bfloat16), dvalue[PROMPT:].reshape(count, width_k).astype(jnp.bfloat16))
            return (carry, emitted)
        zeros = jnp.zeros((PROMPT, HK, HD), jnp.float32)
        start = (zeros, zeros, jnp.zeros((HD,), jnp.float32), jnp.zeros((HD,), jnp.float32))
        final, emitted = lax.scan(one_sample, start, (queries, ckeys, cvalues, grads, lens))
        key_acc, value_acc, gain_query, gain_key = final
        dpk, gkp = norm_back(key_acc, punit, pinv, k_gain)
        return (emitted[0], emitted[1], emitted[2], dpk.reshape(PROMPT, width_k).astype(jnp.bfloat16), value_acc.reshape(PROMPT, width_k).astype(jnp.bfloat16), gain_query, gain_key + gkp)
    items = (prompt_key.reshape(N_DP, PROMPT, width_k), prompt_value.reshape(N_DP, PROMPT, width_k), query.reshape(N_DP, N_GROUP, count, width_q), comp_key.reshape(N_DP, N_GROUP, count, width_k), comp_value.reshape(N_DP, N_GROUP, count, width_k), d_out.reshape(N_DP, N_GROUP, count, width_q), lengths.reshape(N_DP, N_GROUP))
    results = lax.map(one_prompt, items)
    d_query = results[0].reshape(COMP_TOK, width_q)
    d_comp_key = results[1].reshape(COMP_TOK, width_k)
    d_comp_value = results[2].reshape(COMP_TOK, width_k)
    d_prompt_key = results[3].reshape(PROMPT_TOK, width_k)
    d_prompt_value = results[4].reshape(PROMPT_TOK, width_k)
    return (d_query, d_comp_key, d_comp_value, d_prompt_key, d_prompt_value, lax.optimization_barrier(jnp.sum(results[5], axis=0)), lax.optimization_barrier(jnp.sum(results[6], axis=0)))
```

```python
import functools
import math

import jax
import jax.numpy as jnp
from jax import lax
from jax.experimental import pallas as pl
from jax.experimental.pallas import tpu as pltpu
from jax.sharding import PartitionSpec as P

HD = 128
HQ = 32
HK = 4
GROUPS = HQ // HK
EPS = 1e-06
SCALE = HD ** (-0.5)
LOG2E = math.log2(math.e)
MESH = pl.DeviceIdType.MESH
F32 = jnp.float32
BF16 = jnp.bfloat16


def dot_nt(a, b):
    return lax.dot_general(a, b, (((1,), (1,)), ((), ())), preferred_element_type=F32)


def dot_tn(a, b):
    return lax.dot_general(a, b, (((0,), (0,)), ((), ())), preferred_element_type=F32)


def kernel(
    n, nd,
    len_ref, q_hbm, ck_hbm, cv_hbm, pk_hbm, pv_hbm, do_hbm, qg_ref, kg_ref,
    dq_hbm, dck_hbm, dcv_hbm, dpk_hbm, dpv_hbm, gq_ref, gk_ref,
    qv, dov, ckv, vv, pkb, pvb, pf, pvf, uu, kgs, ss, dd, ee, rss, tots, dss, cs, ws, dvs,
    stg, share, rbuf, gbuf, hbuf, dqv, dckv, dcvv, dpkv, dpvv,
    q_sem, do_sem, in_sem, out_sem, dq_sem, pks, pkr, pvs, pvr, shs, shr, gs, gr, hs, hr,
):
    dp = lax.axis_index("dp")
    me = lax.axis_index("group")
    count = q_hbm.shape[0]
    shard = pk_hbm.shape[0]
    plen = shard * n
    width = GROUPS * HD
    total = plen + count

    def peer(k):
        return (dp, lax.rem(me + k, n))

    def dpeer(k):
        return (lax.rem(dp + k, nd), me)

    barrier = pltpu.get_barrier_semaphore()
    for k in range(1, n):
        pl.semaphore_signal(barrier, inc=1, device_id=peer(k), device_id_type=MESH)
    for k in range(1, nd):
        pl.semaphore_signal(barrier, inc=1, device_id=dpeer(k), device_id_type=MESH)

    ins = [
        pltpu.make_async_copy(ck_hbm, ckv, in_sem.at[0]),
        pltpu.make_async_copy(cv_hbm, vv.at[pl.ds(plen, count)], in_sem.at[1]),
        pltpu.make_async_copy(pk_hbm, pkb.at[0], in_sem.at[2]),
        pltpu.make_async_copy(pv_hbm, pvb.at[0], in_sem.at[3]),
    ]
    for c in ins:
        c.start()
    q_in, do_in = [], []
    for g in range(HK):
        cols = pl.ds(g * width, width)
        q_in.append(pltpu.make_async_copy(q_hbm.at[:, cols], qv.at[:, cols], q_sem.at[g]))
        do_in.append(pltpu.make_async_copy(do_hbm.at[:, cols], dov.at[:, cols], do_sem.at[g]))
        q_in[g].start()
        do_in[g].start()

    pl.semaphore_wait(barrier, n - 1 + nd - 1)
    gathers = []
    for k in range(1, n):
        for src, buf, ssem, rsem in ((pk_hbm, pkb, pks, pkr), (pv_hbm, pvb, pvs, pvr)):
            c = pltpu.make_async_remote_copy(
                src_ref=src, dst_ref=buf.at[k], send_sem=ssem.at[k - 1], recv_sem=rsem.at[k - 1],
                device_id=peer(k), device_id_type=MESH)
            c.start()
            gathers.append(c)

    gain = qg_ref[...] * kg_ref[...]

    def key_norm(x):
        return lax.rsqrt(jnp.mean(x * x, axis=-1, keepdims=True) + EPS)

    ins[0].wait()
    ins[1].wait()
    for h in range(HK):
        hc = slice(h * HD, (h + 1) * HD)
        x = ckv[:, hc].astype(F32)
        u = x * key_norm(x)
        uu[plen:total, hc] = u
        kgs[plen:total, hc] = (u * gain).astype(BF16)

    krow = lax.broadcasted_iota(jnp.int32, (count, 2 * HD), 0)
    qcol = lax.broadcasted_iota(jnp.int32, (count, 2 * HD), 1)
    seen = krow <= jnp.where(qcol >= HD, qcol - HD, qcol)
    live = qcol[0:1]
    live = jnp.where(live >= HD, live - HD, live) < len_ref[0]
    ones = jnp.ones((8, HD), BF16)

    def pair(ref, c0):
        return jnp.concatenate([ref[:, c0:c0 + HD], ref[:, c0 + HD:c0 + 2 * HD]], axis=0)

    for g in range(HK):
        hc = slice(g * HD, (g + 1) * HD)
        q_in[g].wait()
        do_in[g].wait()
        for j in range(GROUPS // 2):
            c0 = g * width + j * 2 * HD
            cc = slice(c0, c0 + 2 * HD)
            x = pair(qv, c0)
            go = pair(dov, c0)
            ms = dot_nt(ones, x * x)[0:1]
            r = lax.rsqrt(ms * (1.0 / HD) + EPS)
            rs = r * SCALE
            s = dot_nt(kgs[plen:total, hc], x)
            d = dot_nt(vv[plen:total, hc], go)
            e = jnp.where(seen, jnp.exp2(s * (rs * LOG2E)), 0.0)
            ss[:, cc] = s
            dd[:, cc] = d
            ee[:, cc] = e
            rss[0:1, cc] = r
            tots[0:1, cc] = jnp.sum(e, axis=0, keepdims=True)
            tots[1:2, cc] = jnp.sum(e * d, axis=0, keepdims=True)

    ins[2].wait()
    ins[3].wait()
    for c in gathers:
        c.wait_recv()
    for k in range(n):
        pf[k * shard:(k + 1) * shard, :] = pkb[k].astype(F32)
        pvf[k * shard:(k + 1) * shard, :] = pvb[k].astype(F32)
    for h in range(HK):
        hc = slice(h * HD, (h + 1) * HD)
        x = pf[:, hc]
        u = x * key_norm(x)
        uu[0:plen, hc] = u
        kgs[0:plen, hc] = (u * gain).astype(BF16)
    vv[0:plen, :] = pvf[...].astype(BF16)

    tsum = jnp.zeros((1, HD), F32)
    for g in range(HK):
        hc = slice(g * HD, (g + 1) * HD)
        w = jnp.zeros((total, HD), F32)
        dv = jnp.zeros((total, HD), F32)
        for j in range(GROUPS // 2):
            c0 = g * width + j * 2 * HD
            cc = slice(c0, c0 + 2 * HD)
            x = pair(qv, c0)
            go = pair(dov, c0)
            r = rss[0:1, cc]
            rs = r * SCALE
            sp = dot_nt(kgs[0:plen, hc], x)
            dpr = dot_nt(vv[0:plen, hc], go)
            ep = jnp.exp2(sp * (rs * LOG2E))
            tot = tots[0:1, cc] + jnp.sum(ep, axis=0, keepdims=True)
            t2 = tots[1:2, cc] + jnp.sum(ep * dpr, axis=0, keepdims=True)
            inv = 1.0 / tot
            delta = t2 * inv
            inv = jnp.where(live, inv, 0.0)
            pp = ep * inv
            dsp = pp * ((dpr - delta) * rs)
            pc = ee[:, cc] * inv
            dsc = pc * ((dd[:, cc] - delta) * rs)
            m = (jnp.sum(dsp * sp, axis=0, keepdims=True)
                 + jnp.sum(dsc * ss[:, cc], axis=0, keepdims=True))
            c = r * r * m * (1.0 / HD)
            hh = g * GROUPS + 2 * j
            cs[hh:hh + 1, :] = c[:, 0:HD]
            cs[hh + 1:hh + 2, :] = c[:, HD:2 * HD]
            pw = jnp.concatenate([pp.astype(BF16), pc.astype(BF16)], axis=0)
            ds = jnp.concatenate([dsp.astype(BF16), dsc.astype(BF16)], axis=0)
            dss[:, cc] = ds
            w = w + jnp.dot(ds, x, preferred_element_type=F32)
            dv = dv + jnp.dot(pw, go, preferred_element_type=F32)
        ws[:, hc] = w
        dvs[:, hc] = dv
        tsum = tsum + jnp.sum(w * uu[:, hc], axis=0, keepdims=True)

    gbuf[me] = tsum
    for k in range(n):
        stg[k, 0:shard, :] = ws[k * shard:(k + 1) * shard, :]
        stg[k, shard:2 * shard, :] = dvs[k * shard:(k + 1) * shard, :]
        if k:
            share[k] = stg[k].astype(BF16)
    gains, shares = [], []
    for k in range(1, n):
        c = pltpu.make_async_remote_copy(
            src_ref=gbuf.at[me], dst_ref=gbuf.at[me], send_sem=gs.at[k - 1], recv_sem=gr.at[k - 1],
            device_id=peer(k), device_id_type=MESH)
        c.start()
        gains.append(c)
    for k in range(1, n):
        c = pltpu.make_async_remote_copy(
            src_ref=share.at[k], dst_ref=rbuf.at[k - 1], send_sem=shs.at[k - 1],
            recv_sem=shr.at[k - 1], device_id=peer(n - k), device_id_type=MESH)
        c.start()
        shares.append(c)

    ct = jnp.transpose(cs[...])
    outs = []

    def dq_group(g):
        hc = slice(g * HD, (g + 1) * HD)
        for j in range(GROUPS // 2):
            c0 = g * width + j * 2 * HD
            a = dot_tn(dss[:, c0:c0 + 2 * HD], kgs[:, hc])
            hh = g * GROUPS + 2 * j
            for i in range(2):
                col = slice(c0 + i * HD, c0 + (i + 1) * HD)
                x = qv[:, col].astype(F32)
                dqv[:, col] = (a[i * HD:(i + 1) * HD] - x * ct[:, hh + i:hh + i + 1]).astype(BF16)
        cols = pl.ds(g * width, width)
        c = pltpu.make_async_copy(dqv.at[:, cols], dq_hbm.at[:, cols], dq_sem.at[g])
        c.start()
        outs.append(c)

    for g in range(HK):
        dq_group(g)

    def back(w, u, x):
        a = w * gain
        return key_norm(x) * (a - u * jnp.mean(a * u, axis=-1, keepdims=True))

    for h in range(HK):
        hc = slice(h * HD, (h + 1) * HD)
        x = ckv[:, hc].astype(F32)
        dckv[:, hc] = back(ws[plen:total, hc], uu[plen:total, hc], x).astype(BF16)
    dcvv[...] = dvs[plen:total, :].astype(BF16)
    for i, (src, dst) in enumerate(((dckv, dck_hbm), (dcvv, dcv_hbm))):
        c = pltpu.make_async_copy(src, dst, out_sem.at[i])
        c.start()
        outs.append(c)

    for c in gains:
        c.wait_recv()
    tg = gbuf[0]
    for k in range(1, n):
        tg = tg + gbuf[k]
    hbuf[dp] = tg
    dgains = []
    for k in range(1, nd):
        c = pltpu.make_async_remote_copy(
            src_ref=hbuf.at[dp], dst_ref=hbuf.at[dp], send_sem=hs.at[k - 1], recv_sem=hr.at[k - 1],
            device_id=dpeer(k), device_id_type=MESH)
        c.start()
        dgains.append(c)

    for c in shares:
        c.wait_recv()
    acc = stg[0]
    for k in range(n - 1):
        acc = acc + rbuf[k].astype(F32)
    for h in range(HK):
        hc = slice(h * HD, (h + 1) * HD)
        dx = back(acc[0:shard, hc], uu[0:shard, hc], pf[0:shard, hc])
        dpkv[:, hc] = dx.astype(BF16)
    dpvv[...] = acc[shard:2 * shard].astype(BF16)
    for i, (src, dst) in enumerate(((dpkv, dpk_hbm), (dpvv, dpv_hbm))):
        c = pltpu.make_async_copy(src, dst, out_sem.at[2 + i])
        c.start()
        outs.append(c)

    for c in dgains:
        c.wait_recv()
    tt = hbuf[0]
    for k in range(1, nd):
        tt = tt + hbuf[k]
    gq_ref[...] = tt * kg_ref[...]
    gk_ref[...] = tt * qg_ref[...]
    for c in outs:
        c.wait()
    for c in gathers + gains + shares + dgains:
        c.wait_send()


def local(n, nd, query, comp_key, comp_value, prompt_key, prompt_value, d_out, q_gain, k_gain, lengths):
    count = query.shape[0]
    shard = prompt_key.shape[0]
    plen = shard * n
    total = plen + count
    wq, wk = HQ * HD, HK * HD
    any_spec = pl.BlockSpec(memory_space=pl.ANY)
    vmem = pl.BlockSpec(memory_space=pltpu.VMEM)
    dma = pltpu.SemaphoreType.DMA
    np_, nd_ = max(n - 1, 1), max(nd - 1, 1)
    res = pl.pallas_call(
        functools.partial(kernel, n, nd),
        out_shape=(
            jax.ShapeDtypeStruct((count, wq), BF16),
            jax.ShapeDtypeStruct((count, wk), BF16),
            jax.ShapeDtypeStruct((count, wk), BF16),
            jax.ShapeDtypeStruct((shard, wk), BF16),
            jax.ShapeDtypeStruct((shard, wk), BF16),
            jax.ShapeDtypeStruct((1, HD), F32),
            jax.ShapeDtypeStruct((1, HD), F32),
        ),
        in_specs=[pl.BlockSpec(memory_space=pltpu.SMEM)] + [any_spec] * 6 + [vmem] * 2,
        out_specs=[any_spec] * 5 + [vmem] * 2,
        scratch_shapes=[
            pltpu.VMEM((count, wq), BF16),
            pltpu.VMEM((count, wq), BF16),
            pltpu.VMEM((count, wk), BF16),
            pltpu.VMEM((total, wk), BF16),
            pltpu.VMEM((n, shard, wk), BF16),
            pltpu.VMEM((n, shard, wk), BF16),
            pltpu.VMEM((plen, wk), F32),
            pltpu.VMEM((plen, wk), F32),
            pltpu.VMEM((total, wk), F32),
            pltpu.VMEM((total, wk), BF16),
            pltpu.VMEM((count, wq), F32),
            pltpu.VMEM((count, wq), F32),
            pltpu.VMEM((count, wq), F32),
            pltpu.VMEM((8, wq), F32),
            pltpu.VMEM((8, wq), F32),
            pltpu.VMEM((total, wq), BF16),
            pltpu.VMEM((HQ, HD), F32),
            pltpu.VMEM((total, wk), F32),
            pltpu.VMEM((total, wk), F32),
            pltpu.VMEM((n, 2 * shard, wk), F32),
            pltpu.VMEM((n, 2 * shard, wk), BF16),
            pltpu.VMEM((np_, 2 * shard, wk), BF16),
            pltpu.VMEM((n, 1, HD), F32),
            pltpu.VMEM((nd, 1, HD), F32),
            pltpu.VMEM((count, wq), BF16),
            pltpu.VMEM((count, wk), BF16),
            pltpu.VMEM((count, wk), BF16),
            pltpu.VMEM((shard, wk), BF16),
            pltpu.VMEM((shard, wk), BF16),
            dma((HK,)), dma((HK,)), dma((4,)), dma((4,)), dma((HK,)),
            dma((np_,)), dma((np_,)), dma((np_,)), dma((np_,)),
            dma((np_,)), dma((np_,)), dma((np_,)), dma((np_,)),
            dma((nd_,)), dma((nd_,)),
        ],
        compiler_params=pltpu.CompilerParams(
            collective_id=0, has_side_effects=True, vmem_limit_bytes=48 * 1024 * 1024),
        name="gqa_back",
    )(lengths, query, comp_key, comp_value, prompt_key, prompt_value, d_out,
      q_gain.reshape(1, HD), k_gain.reshape(1, HD))
    return (*res[:5], res[5].reshape(HD), res[6].reshape(HD))


def solution(mesh):
    n, nd = mesh.shape["group"], mesh.shape["dp"]
    row = P(("dp", "group"), None)
    return jax.shard_map(
        functools.partial(local, n, nd),
        mesh=mesh,
        in_specs=(row, row, row, row, row, row, P(), P(), P(("dp", "group"))),
        out_specs=(row, row, row, row, row, P(), P()),
        check_vma=False,
    )
```

```python
import functools
import math

import jax
import jax.numpy as jnp
from jax import lax
from jax.experimental import pallas as pl
from jax.experimental.pallas import tpu as pltpu
from jax.sharding import PartitionSpec as P

HD = 128
HQ = 32
HK = 4
GROUPS = HQ // HK
EPS = 1e-06
SCALE = HD ** (-0.5)
LOG2E = math.log2(math.e)
MESH = pl.DeviceIdType.MESH
F32 = jnp.float32
BF16 = jnp.bfloat16


def dot_nt(a, b):
    return lax.dot_general(a, b, (((1,), (1,)), ((), ())), preferred_element_type=F32)


def dot_tn(a, b):
    return lax.dot_general(a, b, (((0,), (0,)), ((), ())), preferred_element_type=F32)


def kernel(
    n, nd,
    len_hbm, q_hbm, ck_hbm, cv_hbm, pk_hbm, pv_hbm, do_hbm, qg_hbm, kg_hbm,
    dqv, dckv, dcvv, dpkv, dpvv, gq_ref, gk_ref,
    len_ref, qg_ref, kg_ref,
    qv, dov, ckv, vv, pkb, pvb, pf, pvf, uu, kgs, ss, dd, ee, rss, tots, dss, cs, ws, dvs,
    stg, share, rbuf, gbuf, hbuf,
    q_sem, do_sem, in_sem, pks, pkr, pvs, pvr, shs, shr, gs, gr, hs, hr,
):
    dp = lax.axis_index("dp")
    me = lax.axis_index("group")
    count = q_hbm.shape[0]
    shard = pk_hbm.shape[0]
    plen = shard * n
    width = GROUPS * HD
    total = plen + count

    def peer(k):
        return (dp, lax.rem(me + k, n))

    def dpeer(k):
        return (lax.rem(dp + k, nd), me)

    barrier = pltpu.get_barrier_semaphore()
    for k in range(1, n):
        pl.semaphore_signal(barrier, inc=1, device_id=peer(k), device_id_type=MESH)
    for k in range(1, nd):
        pl.semaphore_signal(barrier, inc=1, device_id=dpeer(k), device_id_type=MESH)

    ins = [
        pltpu.make_async_copy(ck_hbm, ckv, in_sem.at[0]),
        pltpu.make_async_copy(cv_hbm, vv.at[pl.ds(plen, count)], in_sem.at[1]),
        pltpu.make_async_copy(pk_hbm, pkb.at[0], in_sem.at[2]),
        pltpu.make_async_copy(pv_hbm, pvb.at[0], in_sem.at[3]),
        pltpu.make_async_copy(qg_hbm, qg_ref, in_sem.at[4]),
        pltpu.make_async_copy(kg_hbm, kg_ref, in_sem.at[5]),
        pltpu.make_async_copy(len_hbm, len_ref, in_sem.at[6]),
    ]
    for c in ins:
        c.start()
    q_in, do_in = [], []
    for g in range(HK):
        cols = pl.ds(g * width, width)
        q_in.append(pltpu.make_async_copy(q_hbm.at[:, cols], qv.at[:, cols], q_sem.at[g]))
        do_in.append(pltpu.make_async_copy(do_hbm.at[:, cols], dov.at[:, cols], do_sem.at[g]))
        q_in[g].start()
        do_in[g].start()

    pl.semaphore_wait(barrier, n - 1 + nd - 1)
    gathers = []
    for k in range(1, n):
        for src, buf, ssem, rsem in ((pk_hbm, pkb, pks, pkr), (pv_hbm, pvb, pvs, pvr)):
            c = pltpu.make_async_remote_copy(
                src_ref=src, dst_ref=buf.at[k], send_sem=ssem.at[k - 1], recv_sem=rsem.at[k - 1],
                device_id=peer(k), device_id_type=MESH)
            c.start()
            gathers.append(c)

    for c in ins[4:]:
        c.wait()
    gain = qg_ref[...] * kg_ref[...]

    def key_norm(x):
        return lax.rsqrt(jnp.mean(x * x, axis=-1, keepdims=True) + EPS)

    ins[0].wait()
    ins[1].wait()
    for h in range(HK):
        hc = slice(h * HD, (h + 1) * HD)
        x = ckv[:, hc].astype(F32)
        u = x * key_norm(x)
        uu[plen:total, hc] = u
        kgs[plen:total, hc] = (u * gain).astype(BF16)

    krow = lax.broadcasted_iota(jnp.int32, (count, 2 * HD), 0)
    qcol = lax.broadcasted_iota(jnp.int32, (count, 2 * HD), 1)
    seen = krow <= jnp.where(qcol >= HD, qcol - HD, qcol)
    live = qcol[0:1]
    live = jnp.where(live >= HD, live - HD, live) < len_ref[0]
    ones = jnp.ones((8, HD), BF16)

    def pair(ref, c0):
        return jnp.concatenate([ref[:, c0:c0 + HD], ref[:, c0 + HD:c0 + 2 * HD]], axis=0)

    for g in range(HK):
        hc = slice(g * HD, (g + 1) * HD)
        q_in[g].wait()
        do_in[g].wait()
        for j in range(GROUPS // 2):
            c0 = g * width + j * 2 * HD
            cc = slice(c0, c0 + 2 * HD)
            x = pair(qv, c0)
            go = pair(dov, c0)
            ms = dot_nt(ones, x * x)[0:1]
            r = lax.rsqrt(ms * (1.0 / HD) + EPS)
            rs = r * SCALE
            s = dot_nt(kgs[plen:total, hc], x)
            d = dot_nt(vv[plen:total, hc], go)
            e = jnp.where(seen, jnp.exp2(s * (rs * LOG2E)), 0.0)
            ss[:, cc] = s
            dd[:, cc] = d
            ee[:, cc] = e
            rss[0:1, cc] = r
            tots[0:1, cc] = jnp.sum(e, axis=0, keepdims=True)
            tots[1:2, cc] = jnp.sum(e * d, axis=0, keepdims=True)

    ins[2].wait()
    ins[3].wait()
    for c in gathers:
        c.wait_recv()
    for k in range(n):
        pf[k * shard:(k + 1) * shard, :] = pkb[k].astype(F32)
        pvf[k * shard:(k + 1) * shard, :] = pvb[k].astype(F32)
    for h in range(HK):
        hc = slice(h * HD, (h + 1) * HD)
        x = pf[:, hc]
        u = x * key_norm(x)
        uu[0:plen, hc] = u
        kgs[0:plen, hc] = (u * gain).astype(BF16)
    vv[0:plen, :] = pvf[...].astype(BF16)

    tsum = jnp.zeros((1, HD), F32)
    for g in range(HK):
        hc = slice(g * HD, (g + 1) * HD)
        w = jnp.zeros((total, HD), F32)
        dv = jnp.zeros((total, HD), F32)
        for j in range(GROUPS // 2):
            c0 = g * width + j * 2 * HD
            cc = slice(c0, c0 + 2 * HD)
            x = pair(qv, c0)
            go = pair(dov, c0)
            r = rss[0:1, cc]
            rs = r * SCALE
            sp = dot_nt(kgs[0:plen, hc], x)
            dpr = dot_nt(vv[0:plen, hc], go)
            ep = jnp.exp2(sp * (rs * LOG2E))
            tot = tots[0:1, cc] + jnp.sum(ep, axis=0, keepdims=True)
            t2 = tots[1:2, cc] + jnp.sum(ep * dpr, axis=0, keepdims=True)
            inv = 1.0 / tot
            delta = t2 * inv
            inv = jnp.where(live, inv, 0.0)
            pp = ep * inv
            dsp = pp * ((dpr - delta) * rs)
            pc = ee[:, cc] * inv
            dsc = pc * ((dd[:, cc] - delta) * rs)
            m = (jnp.sum(dsp * sp, axis=0, keepdims=True)
                 + jnp.sum(dsc * ss[:, cc], axis=0, keepdims=True))
            c = r * r * m * (1.0 / HD)
            hh = g * GROUPS + 2 * j
            cs[hh:hh + 1, :] = c[:, 0:HD]
            cs[hh + 1:hh + 2, :] = c[:, HD:2 * HD]
            pw = jnp.concatenate([pp.astype(BF16), pc.astype(BF16)], axis=0)
            ds = jnp.concatenate([dsp.astype(BF16), dsc.astype(BF16)], axis=0)
            dss[:, cc] = ds
            w = w + jnp.dot(ds, x, preferred_element_type=F32)
            dv = dv + jnp.dot(pw, go, preferred_element_type=F32)
        ws[:, hc] = w
        dvs[:, hc] = dv
        tsum = tsum + jnp.sum(w * uu[:, hc], axis=0, keepdims=True)

    gbuf[me] = tsum
    for k in range(n):
        stg[k, 0:shard, :] = ws[k * shard:(k + 1) * shard, :]
        stg[k, shard:2 * shard, :] = dvs[k * shard:(k + 1) * shard, :]
        if k:
            share[k] = stg[k].astype(BF16)
    gains, shares = [], []
    for k in range(1, n):
        c = pltpu.make_async_remote_copy(
            src_ref=gbuf.at[me], dst_ref=gbuf.at[me], send_sem=gs.at[k - 1], recv_sem=gr.at[k - 1],
            device_id=peer(k), device_id_type=MESH)
        c.start()
        gains.append(c)
    for k in range(1, n):
        c = pltpu.make_async_remote_copy(
            src_ref=share.at[k], dst_ref=rbuf.at[k - 1], send_sem=shs.at[k - 1],
            recv_sem=shr.at[k - 1], device_id=peer(n - k), device_id_type=MESH)
        c.start()
        shares.append(c)

    ct = jnp.transpose(cs[...])

    def dq_group(g):
        hc = slice(g * HD, (g + 1) * HD)
        for j in range(GROUPS // 2):
            c0 = g * width + j * 2 * HD
            a = dot_tn(dss[:, c0:c0 + 2 * HD], kgs[:, hc])
            hh = g * GROUPS + 2 * j
            for i in range(2):
                col = slice(c0 + i * HD, c0 + (i + 1) * HD)
                x = qv[:, col].astype(F32)
                dqv[:, col] = (a[i * HD:(i + 1) * HD] - x * ct[:, hh + i:hh + i + 1]).astype(BF16)

    for g in range(HK):
        dq_group(g)

    def back(w, u, x):
        a = w * gain
        return key_norm(x) * (a - u * jnp.mean(a * u, axis=-1, keepdims=True))

    for h in range(HK):
        hc = slice(h * HD, (h + 1) * HD)
        x = ckv[:, hc].astype(F32)
        dckv[:, hc] = back(ws[plen:total, hc], uu[plen:total, hc], x).astype(BF16)
    dcvv[...] = dvs[plen:total, :].astype(BF16)

    for c in gains:
        c.wait_recv()
    tg = gbuf[0]
    for k in range(1, n):
        tg = tg + gbuf[k]
    hbuf[dp] = tg
    dgains = []
    for k in range(1, nd):
        c = pltpu.make_async_remote_copy(
            src_ref=hbuf.at[dp], dst_ref=hbuf.at[dp], send_sem=hs.at[k - 1], recv_sem=hr.at[k - 1],
            device_id=dpeer(k), device_id_type=MESH)
        c.start()
        dgains.append(c)

    for c in shares:
        c.wait_recv()
    acc = stg[0]
    for k in range(n - 1):
        acc = acc + rbuf[k].astype(F32)
    for h in range(HK):
        hc = slice(h * HD, (h + 1) * HD)
        dx = back(acc[0:shard, hc], uu[0:shard, hc], pf[0:shard, hc])
        dpkv[:, hc] = dx.astype(BF16)
    dpvv[...] = acc[shard:2 * shard].astype(BF16)

    for c in dgains:
        c.wait_recv()
    tt = hbuf[0]
    for k in range(1, nd):
        tt = tt + hbuf[k]
    gq_ref[...] = tt * kg_ref[...]
    gk_ref[...] = tt * qg_ref[...]
    for c in gathers + gains + shares + dgains:
        c.wait_send()


def put_out(*refs):
    sem = refs[14]
    copies = [pltpu.make_async_copy(refs[i], refs[7 + i], sem.at[i]) for i in range(7)]
    for c in copies:
        c.start()
    for c in copies:
        c.wait()


def local(n, nd, query, comp_key, comp_value, prompt_key, prompt_value, d_out, q_gain, k_gain, lengths):
    count = query.shape[0]
    shard = prompt_key.shape[0]
    plen = shard * n
    total = plen + count
    wq, wk = HQ * HD, HK * HD
    hbm = pl.BlockSpec(memory_space=pltpu.HBM)
    vmem = pl.BlockSpec(memory_space=pltpu.VMEM)
    dma = pltpu.SemaphoreType.DMA
    np_, nd_ = max(n - 1, 1), max(nd - 1, 1)
    shapes = (
        jax.ShapeDtypeStruct((count, wq), BF16),
        jax.ShapeDtypeStruct((count, wk), BF16),
        jax.ShapeDtypeStruct((count, wk), BF16),
        jax.ShapeDtypeStruct((shard, wk), BF16),
        jax.ShapeDtypeStruct((shard, wk), BF16),
        jax.ShapeDtypeStruct((1, HD), F32),
        jax.ShapeDtypeStruct((1, HD), F32),
    )
    res = pl.pallas_call(
        functools.partial(kernel, n, nd),
        out_shape=shapes,
        in_specs=[hbm] * 9,
        out_specs=[vmem] * 7,
        scratch_shapes=[
            pltpu.SMEM((1,), jnp.int32),
            pltpu.VMEM((1, HD), F32),
            pltpu.VMEM((1, HD), F32),
            pltpu.VMEM((count, wq), BF16),
            pltpu.VMEM((count, wq), BF16),
            pltpu.VMEM((count, wk), BF16),
            pltpu.VMEM((total, wk), BF16),
            pltpu.VMEM((n, shard, wk), BF16),
            pltpu.VMEM((n, shard, wk), BF16),
            pltpu.VMEM((plen, wk), F32),
            pltpu.VMEM((plen, wk), F32),
            pltpu.VMEM((total, wk), F32),
            pltpu.VMEM((total, wk), BF16),
            pltpu.VMEM((count, wq), F32),
            pltpu.VMEM((count, wq), F32),
            pltpu.VMEM((count, wq), F32),
            pltpu.VMEM((8, wq), F32),
            pltpu.VMEM((8, wq), F32),
            pltpu.VMEM((total, wq), BF16),
            pltpu.VMEM((HQ, HD), F32),
            pltpu.VMEM((total, wk), F32),
            pltpu.VMEM((total, wk), F32),
            pltpu.VMEM((n, 2 * shard, wk), F32),
            pltpu.VMEM((n, 2 * shard, wk), BF16),
            pltpu.VMEM((np_, 2 * shard, wk), BF16),
            pltpu.VMEM((n, 1, HD), F32),
            pltpu.VMEM((nd, 1, HD), F32),
            dma((HK,)), dma((HK,)), dma((7,)),
            dma((np_,)), dma((np_,)), dma((np_,)), dma((np_,)),
            dma((np_,)), dma((np_,)), dma((np_,)), dma((np_,)),
            dma((nd_,)), dma((nd_,)),
        ],
        compiler_params=pltpu.CompilerParams(
            collective_id=0, has_side_effects=True, vmem_limit_bytes=48 * 1024 * 1024),
        name="gqa_back",
    )(lengths, query, comp_key, comp_value, prompt_key, prompt_value, d_out,
      q_gain.reshape(1, HD), k_gain.reshape(1, HD))
    res = pl.pallas_call(
        put_out,
        out_shape=shapes,
        in_specs=[pl.BlockSpec(memory_space=pl.ANY)] * 7,
        out_specs=[hbm] * 7,
        scratch_shapes=[dma((7,))],
        compiler_params=pltpu.CompilerParams(vmem_limit_bytes=1024 * 1024),
        name="put_out",
    )(*res)
    return (*res[:5], res[5].reshape(HD), res[6].reshape(HD))


def solution(mesh):
    n, nd = mesh.shape["group"], mesh.shape["dp"]
    row = P(("dp", "group"), None)
    return jax.shard_map(
        functools.partial(local, n, nd),
        mesh=mesh,
        in_specs=(row, row, row, row, row, row, P(), P(), P(("dp", "group"))),
        out_specs=(row, row, row, row, row, P(), P()),
        check_vma=False,
    )
```

```python
import functools
import math

import jax
import jax.numpy as jnp
from jax import lax
from jax.experimental import pallas as pl
from jax.experimental.pallas import tpu as pltpu
from jax.sharding import PartitionSpec as P

HD = 128
HQ = 32
HK = 4
GROUPS = HQ // HK
EPS = 1e-06
SCALE = HD ** (-0.5)
LOG2E = math.log2(math.e)
MESH = pl.DeviceIdType.MESH
F32 = jnp.float32
BF16 = jnp.bfloat16


def dot_nt(a, b):
    return lax.dot_general(a, b, (((1,), (1,)), ((), ())), preferred_element_type=F32)


def dot_tn(a, b):
    return lax.dot_general(a, b, (((0,), (0,)), ((), ())), preferred_element_type=F32)


def kernel(
    n, nd,
    len_hbm, q_hbm, ck_hbm, cv_hbm, pk_hbm, pv_hbm, do_hbm, qg_hbm, kg_hbm,
    dqv, dckv, dcvv, dpkv, dpvv, gq_ref, gk_ref,
    len_ref, qg_ref, kg_ref,
    qv, dov, ckv, vv, pkb, pvb, pf, pvf, uu, kgs, ss, dd, ee, rss, tots, dss, cs, ws, dvs,
    stg, share, rbuf, gbuf, hbuf,
    q_sem, do_sem, in_sem, pks, pkr, pvs, pvr, shs, shr, gs, gr, hs, hr,
):
    dp = lax.axis_index("dp")
    me = lax.axis_index("group")
    count = q_hbm.shape[0]
    shard = pk_hbm.shape[0]
    plen = shard * n
    width = GROUPS * HD
    total = plen + count

    def peer(k):
        return (dp, lax.rem(me + k, n))

    def dpeer(k):
        return (lax.rem(dp + k, nd), me)

    barrier = pltpu.get_barrier_semaphore()
    for k in range(1, n):
        pl.semaphore_signal(barrier, inc=1, device_id=peer(k), device_id_type=MESH)
    for k in range(1, nd):
        pl.semaphore_signal(barrier, inc=1, device_id=dpeer(k), device_id_type=MESH)

    ins = [
        pltpu.make_async_copy(ck_hbm, ckv, in_sem.at[0]),
        pltpu.make_async_copy(cv_hbm, vv.at[pl.ds(plen, count)], in_sem.at[1]),
        pltpu.make_async_copy(pk_hbm, pkb.at[0], in_sem.at[2]),
        pltpu.make_async_copy(pv_hbm, pvb.at[0], in_sem.at[3]),
        pltpu.make_async_copy(qg_hbm, qg_ref, in_sem.at[4]),
        pltpu.make_async_copy(kg_hbm, kg_ref, in_sem.at[5]),
        pltpu.make_async_copy(len_hbm, len_ref, in_sem.at[6]),
    ]
    for c in ins:
        c.start()
    q_in, do_in = [], []
    for g in range(HK):
        cols = pl.ds(g * width, width)
        q_in.append(pltpu.make_async_copy(q_hbm.at[:, cols], qv.at[:, cols], q_sem.at[g]))
        do_in.append(pltpu.make_async_copy(do_hbm.at[:, cols], dov.at[:, cols], do_sem.at[g]))
        q_in[g].start()
        do_in[g].start()

    pl.semaphore_wait(barrier, n - 1 + nd - 1)
    gathers = []
    for k in range(1, n):
        for src, buf, ssem, rsem in ((pk_hbm, pkb, pks, pkr), (pv_hbm, pvb, pvs, pvr)):
            c = pltpu.make_async_remote_copy(
                src_ref=src, dst_ref=buf.at[k], send_sem=ssem.at[k - 1], recv_sem=rsem.at[k - 1],
                device_id=peer(k), device_id_type=MESH)
            c.start()
            gathers.append(c)

    for c in ins[4:]:
        c.wait()
    gain = qg_ref[...] * kg_ref[...]

    def key_norm(x):
        return lax.rsqrt(jnp.mean(x * x, axis=-1, keepdims=True) + EPS)

    ins[0].wait()
    ins[1].wait()
    for h in range(HK):
        hc = slice(h * HD, (h + 1) * HD)
        x = ckv[:, hc].astype(F32)
        u = x * key_norm(x)
        uu[plen:total, hc] = u
        kgs[plen:total, hc] = (u * gain).astype(BF16)

    krow = lax.broadcasted_iota(jnp.int32, (count, 2 * HD), 0)
    qcol = lax.broadcasted_iota(jnp.int32, (count, 2 * HD), 1)
    seen = krow <= jnp.where(qcol >= HD, qcol - HD, qcol)
    live = qcol[0:1]
    live = jnp.where(live >= HD, live - HD, live) < len_ref[0]
    ones = jnp.ones((8, HD), BF16)

    def pair(ref, c0):
        return jnp.concatenate([ref[:, c0:c0 + HD], ref[:, c0 + HD:c0 + 2 * HD]], axis=0)

    for g in range(HK):
        hc = slice(g * HD, (g + 1) * HD)
        q_in[g].wait()
        do_in[g].wait()
        for j in range(GROUPS // 2):
            c0 = g * width + j * 2 * HD
            cc = slice(c0, c0 + 2 * HD)
            x = pair(qv, c0)
            go = pair(dov, c0)
            ms = dot_nt(ones, x * x)[0:1]
            r = lax.rsqrt(ms * (1.0 / HD) + EPS)
            rs = r * SCALE
            s = dot_nt(kgs[plen:total, hc], x)
            d = dot_nt(vv[plen:total, hc], go)
            e = jnp.where(seen, jnp.exp2(s * (rs * LOG2E)), 0.0)
            ss[:, cc] = s
            dd[:, cc] = d
            ee[:, cc] = e
            rss[0:1, cc] = r
            tots[0:1, cc] = jnp.sum(e, axis=0, keepdims=True)
            tots[1:2, cc] = jnp.sum(e * d, axis=0, keepdims=True)

    ins[2].wait()
    ins[3].wait()
    for c in gathers:
        c.wait_recv()
    for k in range(n):
        pf[k * shard:(k + 1) * shard, :] = pkb[k].astype(F32)
        pvf[k * shard:(k + 1) * shard, :] = pvb[k].astype(F32)
    for h in range(HK):
        hc = slice(h * HD, (h + 1) * HD)
        x = pf[:, hc]
        u = x * key_norm(x)
        uu[0:plen, hc] = u
        kgs[0:plen, hc] = (u * gain).astype(BF16)
    vv[0:plen, :] = pvf[...].astype(BF16)

    tsum = jnp.zeros((1, HD), F32)
    for g in range(HK):
        hc = slice(g * HD, (g + 1) * HD)
        w = jnp.zeros((total, HD), F32)
        dv = jnp.zeros((total, HD), F32)
        for j in range(GROUPS // 2):
            c0 = g * width + j * 2 * HD
            cc = slice(c0, c0 + 2 * HD)
            x = pair(qv, c0)
            go = pair(dov, c0)
            r = rss[0:1, cc]
            rs = r * SCALE
            sp = dot_nt(kgs[0:plen, hc], x)
            dpr = dot_nt(vv[0:plen, hc], go)
            ep = jnp.exp2(sp * (rs * LOG2E))
            tot = tots[0:1, cc] + jnp.sum(ep, axis=0, keepdims=True)
            t2 = tots[1:2, cc] + jnp.sum(ep * dpr, axis=0, keepdims=True)
            inv = 1.0 / tot
            delta = t2 * inv
            inv = jnp.where(live, inv, 0.0)
            pp = ep * inv
            dsp = pp * ((dpr - delta) * rs)
            pc = ee[:, cc] * inv
            dsc = pc * ((dd[:, cc] - delta) * rs)
            m = (jnp.sum(dsp * sp, axis=0, keepdims=True)
                 + jnp.sum(dsc * ss[:, cc], axis=0, keepdims=True))
            c = r * r * m * (1.0 / HD)
            hh = g * GROUPS + 2 * j
            cs[hh:hh + 1, :] = c[:, 0:HD]
            cs[hh + 1:hh + 2, :] = c[:, HD:2 * HD]
            pw = jnp.concatenate([pp.astype(BF16), pc.astype(BF16)], axis=0)
            ds = jnp.concatenate([dsp.astype(BF16), dsc.astype(BF16)], axis=0)
            dss[:, cc] = ds
            w = w + jnp.dot(ds, x, preferred_element_type=F32)
            dv = dv + jnp.dot(pw, go, preferred_element_type=F32)
        ws[:, hc] = w
        dvs[:, hc] = dv
        tsum = tsum + jnp.sum(w * uu[:, hc], axis=0, keepdims=True)

    gbuf[me] = tsum
    for k in range(n):
        stg[k, 0:shard, :] = ws[k * shard:(k + 1) * shard, :]
        stg[k, shard:2 * shard, :] = dvs[k * shard:(k + 1) * shard, :]
        if k:
            share[k] = stg[k].astype(BF16)
    gains, shares = [], []
    for k in range(1, n):
        c = pltpu.make_async_remote_copy(
            src_ref=gbuf.at[me], dst_ref=gbuf.at[me], send_sem=gs.at[k - 1], recv_sem=gr.at[k - 1],
            device_id=peer(k), device_id_type=MESH)
        c.start()
        gains.append(c)
    for k in range(1, n):
        c = pltpu.make_async_remote_copy(
            src_ref=share.at[k], dst_ref=rbuf.at[k - 1], send_sem=shs.at[k - 1],
            recv_sem=shr.at[k - 1], device_id=peer(n - k), device_id_type=MESH)
        c.start()
        shares.append(c)

    ct = jnp.transpose(cs[...])

    def dq_group(g):
        hc = slice(g * HD, (g + 1) * HD)
        for j in range(GROUPS // 2):
            c0 = g * width + j * 2 * HD
            a = dot_tn(dss[:, c0:c0 + 2 * HD], kgs[:, hc])
            hh = g * GROUPS + 2 * j
            for i in range(2):
                col = slice(c0 + i * HD, c0 + (i + 1) * HD)
                x = qv[:, col].astype(F32)
                dqv[:, col] = (a[i * HD:(i + 1) * HD] - x * ct[:, hh + i:hh + i + 1]).astype(BF16)

    for g in range(HK):
        dq_group(g)

    def back(w, u, x):
        a = w * gain
        return key_norm(x) * (a - u * jnp.mean(a * u, axis=-1, keepdims=True))

    for h in range(HK):
        hc = slice(h * HD, (h + 1) * HD)
        x = ckv[:, hc].astype(F32)
        dckv[:, hc] = back(ws[plen:total, hc], uu[plen:total, hc], x).astype(BF16)
    dcvv[...] = dvs[plen:total, :].astype(BF16)

    for c in gains:
        c.wait_recv()
    tg = gbuf[0]
    for k in range(1, n):
        tg = tg + gbuf[k]
    hbuf[dp] = tg
    dgains = []
    for k in range(1, nd):
        c = pltpu.make_async_remote_copy(
            src_ref=hbuf.at[dp], dst_ref=hbuf.at[dp], send_sem=hs.at[k - 1], recv_sem=hr.at[k - 1],
            device_id=dpeer(k), device_id_type=MESH)
        c.start()
        dgains.append(c)

    for c in shares:
        c.wait_recv()
    acc = stg[0]
    for k in range(n - 1):
        acc = acc + rbuf[k].astype(F32)
    for h in range(HK):
        hc = slice(h * HD, (h + 1) * HD)
        dx = back(acc[0:shard, hc], uu[0:shard, hc], pf[0:shard, hc])
        dpkv[:, hc] = dx.astype(BF16)
    dpvv[...] = acc[shard:2 * shard].astype(BF16)

    for c in dgains:
        c.wait_recv()
    tt = hbuf[0]
    for k in range(1, nd):
        tt = tt + hbuf[k]
    gq_ref[...] = tt * kg_ref[...]
    gk_ref[...] = tt * qg_ref[...]
    for c in gathers + gains + shares + dgains:
        c.wait_send()


def put_out(*refs):
    sem = refs[14]
    copies = [pltpu.make_async_copy(refs[i], refs[7 + i], sem.at[i]) for i in range(7)]
    for c in copies:
        c.start()
    for c in copies:
        c.wait()


def local(n, nd, query, comp_key, comp_value, prompt_key, prompt_value, d_out, q_gain, k_gain, lengths):
    count = query.shape[0]
    shard = prompt_key.shape[0]
    plen = shard * n
    total = plen + count
    wq, wk = HQ * HD, HK * HD
    hbm = pl.BlockSpec(memory_space=pltpu.HBM)
    vmem = pl.BlockSpec(memory_space=pltpu.VMEM)
    dma = pltpu.SemaphoreType.DMA
    np_, nd_ = max(n - 1, 1), max(nd - 1, 1)
    shapes = (
        jax.ShapeDtypeStruct((count, wq), BF16),
        jax.ShapeDtypeStruct((count, wk), BF16),
        jax.ShapeDtypeStruct((count, wk), BF16),
        jax.ShapeDtypeStruct((shard, wk), BF16),
        jax.ShapeDtypeStruct((shard, wk), BF16),
        jax.ShapeDtypeStruct((1, HD), F32),
        jax.ShapeDtypeStruct((1, HD), F32),
    )
    res = pl.pallas_call(
        functools.partial(kernel, n, nd),
        out_shape=shapes,
        in_specs=[hbm] * 9,
        out_specs=[vmem] * 7,
        scratch_shapes=[
            pltpu.SMEM((1,), jnp.int32),
            pltpu.VMEM((1, HD), F32),
            pltpu.VMEM((1, HD), F32),
            pltpu.VMEM((count, wq), BF16),
            pltpu.VMEM((count, wq), BF16),
            pltpu.VMEM((count, wk), BF16),
            pltpu.VMEM((total, wk), BF16),
            pltpu.VMEM((n, shard, wk), BF16),
            pltpu.VMEM((n, shard, wk), BF16),
            pltpu.VMEM((plen, wk), F32),
            pltpu.VMEM((plen, wk), F32),
            pltpu.VMEM((total, wk), F32),
            pltpu.VMEM((total, wk), BF16),
            pltpu.VMEM((count, wq), F32),
            pltpu.VMEM((count, wq), F32),
            pltpu.VMEM((count, wq), F32),
            pltpu.VMEM((8, wq), F32),
            pltpu.VMEM((8, wq), F32),
            pltpu.VMEM((total, wq), BF16),
            pltpu.VMEM((HQ, HD), F32),
            pltpu.VMEM((total, wk), F32),
            pltpu.VMEM((total, wk), F32),
            pltpu.VMEM((n, 2 * shard, wk), F32),
            pltpu.VMEM((n, 2 * shard, wk), BF16),
            pltpu.VMEM((np_, 2 * shard, wk), BF16),
            pltpu.VMEM((n, 1, HD), F32),
            pltpu.VMEM((nd, 1, HD), F32),
            dma((HK,)), dma((HK,)), dma((7,)),
            dma((np_,)), dma((np_,)), dma((np_,)), dma((np_,)),
            dma((np_,)), dma((np_,)), dma((np_,)), dma((np_,)),
            dma((nd_,)), dma((nd_,)),
        ],
        compiler_params=pltpu.CompilerParams(
            collective_id=0, has_side_effects=True, vmem_limit_bytes=48 * 1024 * 1024),
        name="gqa_back",
    )(lengths, *(pltpu.with_memory_space_constraint(a, pltpu.HBM) for a in (
        query, comp_key, comp_value, prompt_key, prompt_value, d_out,
        q_gain.reshape(1, HD), k_gain.reshape(1, HD))))
    res = pl.pallas_call(
        put_out,
        out_shape=shapes,
        in_specs=[pl.BlockSpec(memory_space=pl.ANY)] * 7,
        out_specs=[hbm] * 7,
        scratch_shapes=[dma((7,))],
        compiler_params=pltpu.CompilerParams(vmem_limit_bytes=1024 * 1024),
        name="put_out",
    )(*res)
    return (*res[:5], res[5].reshape(HD), res[6].reshape(HD))


def solution(mesh):
    n, nd = mesh.shape["group"], mesh.shape["dp"]
    row = P(("dp", "group"), None)
    return jax.shard_map(
        functools.partial(local, n, nd),
        mesh=mesh,
        in_specs=(row, row, row, row, row, row, P(), P(), P(("dp", "group"))),
        out_specs=(row, row, row, row, row, P(), P()),
        check_vma=False,
    )
```

```python
import functools
import math

import jax
import jax.numpy as jnp
from jax import lax
from jax.experimental import pallas as pl
from jax.experimental.pallas import tpu as pltpu
from jax.sharding import PartitionSpec as P

HD = 128
HQ = 32
HK = 4
GROUPS = HQ // HK
EPS = 1e-06
SCALE = HD ** (-0.5)
LOG2E = math.log2(math.e)
MESH = pl.DeviceIdType.MESH
F32 = jnp.float32
BF16 = jnp.bfloat16


def dot_nt(a, b):
    return lax.dot_general(a, b, (((1,), (1,)), ((), ())), preferred_element_type=F32)


def dot_tn(a, b):
    return lax.dot_general(a, b, (((0,), (0,)), ((), ())), preferred_element_type=F32)


def kernel(
    n, nd,
    len_hbm, q_hbm, ck_hbm, cv_hbm, pk_hbm, pv_hbm, do_hbm, qg_hbm, kg_hbm,
    dqv, dckv, dcvv, dpkv, dpvv, gq_ref, gk_ref,
    len_ref, qg_ref, kg_ref,
    qv, dov, ckv, vv, pkb, pvb, pf, pvf, uu, kgs, dd, ee, sums, pws, dss, cs, ws, dvs,
    stg, share, rbuf, gbuf, hbuf,
    q_sem, do_sem, in_sem, pks, pkr, pvs, pvr, shs, shr, gs, gr, hs, hr,
):
    dp = lax.axis_index("dp")
    me = lax.axis_index("group")
    count = q_hbm.shape[0]
    shard = pk_hbm.shape[0]
    plen = shard * n
    width = GROUPS * HD
    total = plen + count

    def peer(k):
        return (dp, lax.rem(me + k, n))

    def dpeer(k):
        return (lax.rem(dp + k, nd), me)

    barrier = pltpu.get_barrier_semaphore()
    for k in range(1, n):
        pl.semaphore_signal(barrier, inc=1, device_id=peer(k), device_id_type=MESH)
    for k in range(1, nd):
        pl.semaphore_signal(barrier, inc=1, device_id=dpeer(k), device_id_type=MESH)

    ins = [
        pltpu.make_async_copy(ck_hbm, ckv, in_sem.at[0]),
        pltpu.make_async_copy(cv_hbm, vv.at[pl.ds(plen, count)], in_sem.at[1]),
        pltpu.make_async_copy(pk_hbm, pkb.at[0], in_sem.at[2]),
        pltpu.make_async_copy(pv_hbm, pvb.at[0], in_sem.at[3]),
        pltpu.make_async_copy(qg_hbm, qg_ref, in_sem.at[4]),
        pltpu.make_async_copy(kg_hbm, kg_ref, in_sem.at[5]),
        pltpu.make_async_copy(len_hbm, len_ref, in_sem.at[6]),
    ]
    for c in ins:
        c.start()
    q_in, do_in = [], []
    for g in range(HK):
        cols = pl.ds(g * width, width)
        q_in.append(pltpu.make_async_copy(q_hbm.at[:, cols], qv.at[:, cols], q_sem.at[g]))
        do_in.append(pltpu.make_async_copy(do_hbm.at[:, cols], dov.at[:, cols], do_sem.at[g]))
        q_in[g].start()
        do_in[g].start()

    ins[2].wait()
    ins[3].wait()
    pl.semaphore_wait(barrier, n - 1 + nd - 1)
    gathers = []
    for k in range(1, n):
        for buf, ssem, rsem in ((pkb, pks, pkr), (pvb, pvs, pvr)):
            c = pltpu.make_async_remote_copy(
                src_ref=buf.at[0], dst_ref=buf.at[k], send_sem=ssem.at[k - 1], recv_sem=rsem.at[k - 1],
                device_id=peer(k), device_id_type=MESH)
            c.start()
            gathers.append(c)

    for c in ins[4:]:
        c.wait()
    gain = qg_ref[...] * kg_ref[...]

    def key_norm(x):
        return lax.rsqrt(jnp.mean(x * x, axis=-1, keepdims=True) + EPS)

    ins[0].wait()
    ins[1].wait()
    for h in range(HK):
        hc = slice(h * HD, (h + 1) * HD)
        x = ckv[:, hc].astype(F32)
        u = x * key_norm(x)
        uu[plen:total, hc] = u
        kgs[plen:total, hc] = (u * gain).astype(BF16)

    krow = lax.broadcasted_iota(jnp.int32, (count, 2 * HD), 0)
    qcol = lax.broadcasted_iota(jnp.int32, (count, 2 * HD), 1)
    seen = krow <= jnp.where(qcol >= HD, qcol - HD, qcol)
    ones = jnp.ones((8, HD), BF16)

    def pair(ref, c0):
        return jnp.concatenate([ref[:, c0:c0 + HD], ref[:, c0 + HD:c0 + 2 * HD]], axis=0)

    for g in range(HK):
        hc = slice(g * HD, (g + 1) * HD)
        q_in[g].wait()
        do_in[g].wait()
        for j in range(GROUPS // 2):
            c0 = g * width + j * 2 * HD
            cc = slice(c0, c0 + 2 * HD)
            x = pair(qv, c0)
            go = pair(dov, c0)
            ms = dot_nt(ones, x * x)[0:1]
            r = lax.rsqrt(ms * (1.0 / HD) + EPS)
            rs = r * SCALE
            s = dot_nt(kgs[plen:total, hc], x)
            d = dot_nt(vv[plen:total, hc], go)
            e = jnp.where(seen, jnp.exp2(s * (rs * LOG2E)), 0.0)
            d = d * rs
            ed = e * d
            ee[:, cc] = e.astype(BF16)
            dd[:, cc] = d.astype(BF16)
            sums[0:1, cc] = r
            sums[1:2, cc] = jnp.sum(e, axis=0, keepdims=True)
            sums[2:3, cc] = jnp.sum(ed, axis=0, keepdims=True)
            sums[3:4, cc] = jnp.sum(e * s, axis=0, keepdims=True)
            sums[4:5, cc] = jnp.sum(ed * s, axis=0, keepdims=True)

    for c in gathers:
        c.wait_recv()
    for k in range(n):
        pf[k * shard:(k + 1) * shard, :] = pkb[k].astype(F32)
        pvf[k * shard:(k + 1) * shard, :] = pvb[k].astype(F32)
    for h in range(HK):
        hc = slice(h * HD, (h + 1) * HD)
        x = pf[:, hc]
        u = x * key_norm(x)
        uu[0:plen, hc] = u
        kgs[0:plen, hc] = (u * gain).astype(BF16)
    vv[0:plen, :] = pvf[...].astype(BF16)

    def heads(ref, g):
        return jnp.concatenate(
            [ref[:, g * width + i * HD:g * width + (i + 1) * HD] for i in range(GROUPS)], axis=0)

    slot = lax.rem(lax.broadcasted_iota(jnp.int32, (1, width), 1), HD)
    live = slot < len_ref[0]
    for g in range(HK):
        hc = slice(g * HD, (g + 1) * HD)
        gc = slice(g * width, (g + 1) * width)
        r = sums[0:1, gc]
        rs = r * SCALE
        sp = dot_nt(kgs[0:plen, hc], heads(qv, g))
        dpr = dot_nt(vv[0:plen, hc], heads(dov, g)) * rs
        ep = jnp.exp2(sp * (rs * LOG2E))
        ed = ep * dpr
        tot = sums[1:2, gc] + jnp.sum(ep, axis=0, keepdims=True)
        t2 = sums[2:3, gc] + jnp.sum(ed, axis=0, keepdims=True)
        m1 = sums[3:4, gc] + jnp.sum(ep * sp, axis=0, keepdims=True)
        m2 = sums[4:5, gc] + jnp.sum(ed * sp, axis=0, keepdims=True)
        inv = 1.0 / tot
        delta = t2 * inv
        inv = jnp.where(live, inv, 0.0)
        c = r * r * inv * (m2 - delta * m1) * (1.0 / HD)
        for i in range(GROUPS):
            cs[g * GROUPS + i:g * GROUPS + i + 1, :] = c[:, i * HD:(i + 1) * HD]
        pp = ep * inv
        pws[0:plen, gc] = pp.astype(BF16)
        dss[0:plen, gc] = (pp * (dpr - delta)).astype(BF16)
        sums[5:6, gc] = inv
        sums[6:7, gc] = delta

    tsum = jnp.zeros((1, HD), F32)
    for g in range(HK):
        hc = slice(g * HD, (g + 1) * HD)
        gc = slice(g * width, (g + 1) * width)
        inv = jnp.broadcast_to(sums[5:6, gc], (16, width)).astype(BF16)[None]
        delta = jnp.broadcast_to(sums[6:7, gc], (16, width)).astype(BF16)[None]
        pc = ee[:, gc].reshape(count // 16, 16, width) * inv
        dsc = pc * (dd[:, gc].reshape(count // 16, 16, width) - delta)
        pws[plen:total, gc] = pc.reshape(count, width)
        dss[plen:total, gc] = dsc.reshape(count, width)
        w = jnp.dot(dss[:, gc], heads(qv, g), preferred_element_type=F32)
        dv = jnp.dot(pws[:, gc], heads(dov, g), preferred_element_type=F32)
        ws[:, hc] = w
        dvs[:, hc] = dv
        tsum = tsum + jnp.sum(w * uu[:, hc], axis=0, keepdims=True)

    gbuf[me] = tsum
    for k in range(n):
        stg[k, 0:shard, :] = ws[k * shard:(k + 1) * shard, :]
        stg[k, shard:2 * shard, :] = dvs[k * shard:(k + 1) * shard, :]
        if k:
            share[k] = stg[k].astype(BF16)
    gains, shares = [], []
    for k in range(1, n):
        c = pltpu.make_async_remote_copy(
            src_ref=gbuf.at[me], dst_ref=gbuf.at[me], send_sem=gs.at[k - 1], recv_sem=gr.at[k - 1],
            device_id=peer(k), device_id_type=MESH)
        c.start()
        gains.append(c)
    for k in range(1, n):
        c = pltpu.make_async_remote_copy(
            src_ref=share.at[k], dst_ref=rbuf.at[k - 1], send_sem=shs.at[k - 1],
            recv_sem=shr.at[k - 1], device_id=peer(n - k), device_id_type=MESH)
        c.start()
        shares.append(c)

    ct = jnp.transpose(cs[...])

    def dq_group(g):
        hc = slice(g * HD, (g + 1) * HD)
        for j in range(GROUPS // 2):
            c0 = g * width + j * 2 * HD
            a = dot_tn(dss[:, c0:c0 + 2 * HD], kgs[:, hc])
            hh = g * GROUPS + 2 * j
            for i in range(2):
                col = slice(c0 + i * HD, c0 + (i + 1) * HD)
                x = qv[:, col].astype(F32)
                dqv[:, col] = (a[i * HD:(i + 1) * HD] - x * ct[:, hh + i:hh + i + 1]).astype(BF16)

    for g in range(HK):
        dq_group(g)

    def back(w, u, x):
        a = w * gain
        return key_norm(x) * (a - u * jnp.mean(a * u, axis=-1, keepdims=True))

    for h in range(HK):
        hc = slice(h * HD, (h + 1) * HD)
        x = ckv[:, hc].astype(F32)
        dckv[:, hc] = back(ws[plen:total, hc], uu[plen:total, hc], x).astype(BF16)
    dcvv[...] = dvs[plen:total, :].astype(BF16)

    for c in gains:
        c.wait_recv()
    tg = gbuf[0]
    for k in range(1, n):
        tg = tg + gbuf[k]
    hbuf[dp] = tg
    dgains = []
    for k in range(1, nd):
        c = pltpu.make_async_remote_copy(
            src_ref=hbuf.at[dp], dst_ref=hbuf.at[dp], send_sem=hs.at[k - 1], recv_sem=hr.at[k - 1],
            device_id=dpeer(k), device_id_type=MESH)
        c.start()
        dgains.append(c)

    for c in shares:
        c.wait_recv()
    acc = stg[0]
    for k in range(n - 1):
        acc = acc + rbuf[k].astype(F32)
    for h in range(HK):
        hc = slice(h * HD, (h + 1) * HD)
        dx = back(acc[0:shard, hc], uu[0:shard, hc], pf[0:shard, hc])
        dpkv[:, hc] = dx.astype(BF16)
    dpvv[...] = acc[shard:2 * shard].astype(BF16)

    for c in dgains:
        c.wait_recv()
    tt = hbuf[0]
    for k in range(1, nd):
        tt = tt + hbuf[k]
    gq_ref[...] = tt * kg_ref[...]
    gk_ref[...] = tt * qg_ref[...]
    for c in gathers + gains + shares + dgains:
        c.wait_send()


CUTS = 8


def put_out(*refs):
    sem = refs[14]
    rows = refs[0].shape[0] // CUTS
    parts = [(refs[0].at[pl.ds(i * rows, rows)], refs[7].at[pl.ds(i * rows, rows)]) for i in range(CUTS)]
    parts += list(zip(refs[1:7], refs[8:14]))
    copies = [pltpu.make_async_copy(a, b, sem.at[i]) for i, (a, b) in enumerate(parts)]
    for c in copies:
        c.start()
    for c in copies:
        c.wait()


def local(n, nd, query, comp_key, comp_value, prompt_key, prompt_value, d_out, q_gain, k_gain, lengths):
    count = query.shape[0]
    shard = prompt_key.shape[0]
    plen = shard * n
    total = plen + count
    wq, wk = HQ * HD, HK * HD
    hbm = pl.BlockSpec(memory_space=pltpu.HBM)
    vmem = pl.BlockSpec(memory_space=pltpu.VMEM)
    dma = pltpu.SemaphoreType.DMA
    np_, nd_ = max(n - 1, 1), max(nd - 1, 1)
    shapes = (
        jax.ShapeDtypeStruct((count, wq), BF16),
        jax.ShapeDtypeStruct((count, wk), BF16),
        jax.ShapeDtypeStruct((count, wk), BF16),
        jax.ShapeDtypeStruct((shard, wk), BF16),
        jax.ShapeDtypeStruct((shard, wk), BF16),
        jax.ShapeDtypeStruct((1, HD), F32),
        jax.ShapeDtypeStruct((1, HD), F32),
    )
    res = pl.pallas_call(
        functools.partial(kernel, n, nd),
        out_shape=shapes,
        in_specs=[hbm] * 9,
        out_specs=[vmem] * 7,
        scratch_shapes=[
            pltpu.SMEM((1,), jnp.int32),
            pltpu.VMEM((1, HD), F32),
            pltpu.VMEM((1, HD), F32),
            pltpu.VMEM((count, wq), BF16),
            pltpu.VMEM((count, wq), BF16),
            pltpu.VMEM((count, wk), BF16),
            pltpu.VMEM((total, wk), BF16),
            pltpu.VMEM((n, shard, wk), BF16),
            pltpu.VMEM((n, shard, wk), BF16),
            pltpu.VMEM((plen, wk), F32),
            pltpu.VMEM((plen, wk), F32),
            pltpu.VMEM((total, wk), F32),
            pltpu.VMEM((total, wk), BF16),
            pltpu.VMEM((count, wq), BF16),
            pltpu.VMEM((count, wq), BF16),
            pltpu.VMEM((8, wq), F32),
            pltpu.VMEM((total, wq), BF16),
            pltpu.VMEM((total, wq), BF16),
            pltpu.VMEM((HQ, HD), F32),
            pltpu.VMEM((total, wk), F32),
            pltpu.VMEM((total, wk), F32),
            pltpu.VMEM((n, 2 * shard, wk), F32),
            pltpu.VMEM((n, 2 * shard, wk), BF16),
            pltpu.VMEM((np_, 2 * shard, wk), BF16),
            pltpu.VMEM((n, 1, HD), F32),
            pltpu.VMEM((nd, 1, HD), F32),
            dma((HK,)), dma((HK,)), dma((7,)),
            dma((np_,)), dma((np_,)), dma((np_,)), dma((np_,)),
            dma((np_,)), dma((np_,)), dma((np_,)), dma((np_,)),
            dma((nd_,)), dma((nd_,)),
        ],
        compiler_params=pltpu.CompilerParams(
            collective_id=0, has_side_effects=True, vmem_limit_bytes=48 * 1024 * 1024),
        name="gqa_back",
    )(lengths, *(pltpu.with_memory_space_constraint(a, pltpu.HBM) for a in (
        query, comp_key, comp_value, prompt_key, prompt_value, d_out,
        q_gain.reshape(1, HD), k_gain.reshape(1, HD))))
    res = pl.pallas_call(
        put_out,
        out_shape=shapes,
        in_specs=[pl.BlockSpec(memory_space=pl.ANY)] * 7,
        out_specs=[hbm] * 7,
        scratch_shapes=[dma((6 + CUTS,))],
        compiler_params=pltpu.CompilerParams(vmem_limit_bytes=1024 * 1024),
        name="put_out",
    )(*res)
    return (*res[:5], res[5].reshape(HD), res[6].reshape(HD))


def solution(mesh):
    n, nd = mesh.shape["group"], mesh.shape["dp"]
    row = P(("dp", "group"), None)
    return jax.shard_map(
        functools.partial(local, n, nd),
        mesh=mesh,
        in_specs=(row, row, row, row, row, row, P(), P(), P(("dp", "group"))),
        out_specs=(row, row, row, row, row, P(), P()),
        check_vma=False,
    )
```
